32 devices in a mesh: dp: 4 (over y, x), mp: 8 (over z, core).
Axes of the slice: x: 2, y: 2, z: 4, core: 2. Of those that a mesh axis runs over, the one named last changes fastest.
Arguments:
- tokens: bfloat16 [1024, 4096], P('dp'), may hold values from -96 to 96
- inner_weight: float32 [2, 4096, 16384], P(None, 'dp', 'mp'), may hold values from -5 to 5, as said below
- inner_grad: float32 [2, 4096, 16384], P(None, 'dp', 'mp'), may hold values from -400 to 400
- inner_row: float32 [2, 4096], P(None, 'dp'), may hold values from 0.01 to 1
- inner_col: float32 [2, 16384], P(None, 'mp'), may hold values from 0.01 to 1
- outer_weight: float32 [16384, 4096], P('mp', 'dp'), may hold values from -5 to 5, as said below
- outer_grad: float32 [16384, 4096], P('mp', 'dp'), may hold values from -400 to 400
- outer_row: float32 [16384], P('mp'), may hold values from 0.01 to 1
- outer_col: float32 [4096], P('dp'), may hold values from 0.01 to 1
Outputs:
- inner_new: float32 [2, 4096, 16384], P(None, 'dp', 'mp')
- inner_update: float32 [2, 4096, 16384], P(None, 'dp', 'mp')
- inner_row_new: float32 [2, 4096], P(None, 'dp')
- inner_col_new: float32 [2, 16384], P(None, 'mp')
- outer_new: float32 [16384, 4096], P('mp', 'dp')
- outer_update: float32 [16384, 4096], P('mp', 'dp')
- outer_row_new: float32 [16384], P('mp')
- outer_col_new: float32 [4096], P('dp')
- hidden: bfloat16 [1024, 16384], P('dp', 'mp')
The draws below stay inside these ranges and needn't reach their ends.
Inputs may be any that keep to these rules, and one draw needn't show every extreme that they name: `inner_weight`: parameters of the gate and up projections. `outer_weight`: parameters of the down projection.
All inputs are finite; a program needn't handle non-finite values.
Results may differ from the reference program's by a relative error of at most 0.0058.
Values may be sent and summed in bfloat16 or wider, within the bound.
No kernel may reach another device: no remote copies, remote signals or barrier semaphores. Data moves between devices by JAX's collectives and lax.ppermute only.
A program may use at most 192 MiB of HBM per device.

```python
import math
import jax
import jax.numpy as jnp
from jax import lax

D = 4096
FF = 16384
STEP = 10
TOKENS = 1024


def scaled_field(key, leading, row_count, col_count):
    subkeys = jax.random.split(key, 3)
    row_scale = jnp.exp(jax.random.uniform(subkeys[0], (leading, row_count, 1), jnp.float32, math.log(0.3), math.log(3.0)))
    col_scale = jnp.exp(jax.random.uniform(subkeys[1], (leading, 1, col_count), jnp.float32, math.log(0.3), math.log(3.0)))
    row_ramp = 1.0 + 2.0 * jnp.arange(row_count, dtype=jnp.float32)[None, :, None] / (row_count - 1)
    col_ramp = 1.0 + 2.0 * jnp.arange(col_count, dtype=jnp.float32)[None, None, :] / (col_count - 1)
    pattern = jnp.clip(jax.random.normal(subkeys[2], (leading, row_count, col_count), jnp.float32), -4.0, 4.0)
    return pattern * row_scale * col_scale * row_ramp * col_ramp


def weight_field(key, leading, row_count, col_count, fan_in):
    subkeys = jax.random.split(key, 3)
    row_scale = jnp.exp(jax.random.uniform(subkeys[0], (leading, row_count, 1), jnp.float32, math.log(0.3), math.log(3.0)))
    col_scale = jnp.exp(jax.random.uniform(subkeys[1], (leading, 1, col_count), jnp.float32, math.log(0.3), math.log(3.0)))
    row_ramp = 1.0 + 0.732 * jnp.arange(row_count, dtype=jnp.float32)[None, :, None] / (row_count - 1)
    col_ramp = 1.0 + 0.732 * jnp.arange(col_count, dtype=jnp.float32)[None, None, :] / (col_count - 1)
    pattern = jnp.clip(jax.random.normal(subkeys[2], (leading, row_count, col_count), jnp.float32), -4.0, 4.0)
    return pattern * row_scale * col_scale * row_ramp * col_ramp * (0.3 / math.sqrt(fan_in))


def draw_tokens(key, part):
    base_key = jax.random.fold_in(key, 43)
    base = jnp.clip(jax.random.normal(base_key, (TOKENS, D), jnp.float32), -6.0, 6.0)
    feature_gain = jnp.where(jnp.arange(D) < D // 4, 16.0, 1.0).astype(jnp.float32)
    return (base * feature_gain[None, :]).astype(jnp.bfloat16)


def draw_inner_grad(key, part):
    field = scaled_field(jax.random.fold_in(key, 11), 2, D, FF)
    subkeys = jax.random.split(jax.random.fold_in(key, 13), 2)
    row_flag = jax.random.randint(subkeys[0], (D, 1), 0, 2).astype(jnp.float32)
    col_flag = jax.random.randint(subkeys[1], (1, FF), 0, 2).astype(jnp.float32)
    interplay = 0.1 + 0.9 * row_flag * col_flag
    gate_grad = field[0] * interplay
    up_grad = field[1] * 0.002
    return jnp.stack([gate_grad, up_grad], axis=0)


def draw_outer_grad(key, part):
    return scaled_field(jax.random.fold_in(key, 23), 1, FF, D)[0]


def draw_inner_weight(key, part):
    field = weight_field(jax.random.fold_in(key, 31), 2, D, FF, D)
    row_gain = jnp.where(jnp.arange(D) < D // 4, 0.01, 1.0).astype(jnp.float32)
    return field * row_gain[None, :, None]


def draw_outer_weight(key, part):
    return weight_field(jax.random.fold_in(key, 37), 1, FF, D, FF)[0]


def levels(rng, dims, cuts, smallest, top_value):
    gain, own = 1.0, jax.random.fold_in(rng, 6)
    for position, blocks in cuts:
        steps = jnp.exp(jax.random.uniform(jax.random.fold_in(own, position), (blocks,), jnp.float32, smallest / len(cuts), top_value / len(cuts)))
        gain = gain * jnp.repeat(steps, dims[position] // blocks).reshape([-1 if axis == position else 1 for axis in range(len(dims))])
    return gain


def setup_inputs(seed: int = 0) -> dict:
    splits = jax.random.split(jax.random.key(seed), 10)
    tokens = draw_tokens(jax.random.fold_in(splits[9], 71), 0)
    inner_weight = draw_inner_weight(jax.random.fold_in(splits[9], 71), 0)
    inner_grad = draw_inner_grad(jax.random.fold_in(splits[9], 71), 0)
    inner_row = jnp.clip(jnp.exp(math.log(1.0) - 4.6051702 * jax.random.uniform(splits[3], (2, D), jnp.float32) ** levels(splits[3], (2, D), ((1, 4),), -0.2, 0.2)), 0.01, 1.0)
    inner_col = jnp.clip(jnp.exp(math.log(1.0) - 4.6051702 * jax.random.uniform(splits[4], (2, FF), jnp.float32) ** levels(splits[4], (2, FF), ((1, 8),), -0.2, 0.2)), 0.01, 1.0)
    outer_weight = draw_outer_weight(jax.random.fold_in(splits[9], 71), 0)
    outer_grad = draw_outer_grad(jax.random.fold_in(splits[9], 71), 0)
    outer_row = jnp.clip(jnp.exp(math.log(1.0) - 4.6051702 * jax.random.uniform(splits[7], (FF,), jnp.float32) ** levels(splits[7], (FF,), ((0, 8),), -0.2, 0.2)), 0.01, 1.0)
    outer_col = jnp.clip(jnp.exp(math.log(1.0) - 4.6051702 * jax.random.uniform(splits[8], (D,), jnp.float32) ** levels(splits[8], (D,), ((0, 4),), -0.2, 0.2)), 0.01, 1.0)
    return {"tokens": tokens, "inner_weight": inner_weight, "inner_grad": inner_grad, "inner_row": inner_row, "inner_col": inner_col, "outer_weight": outer_weight, "outer_grad": outer_grad, "outer_row": outer_row, "outer_col": outer_col}


def factor_update(param, grad, row, col):
    forget = 1.0 - STEP ** (-0.8)
    relative = min(0.01, STEP ** (-0.5))
    square = grad * grad + 1e-30
    row_new = forget * row + (1.0 - forget) * lax.optimization_barrier(jnp.mean(square, axis=-1))
    col_new = forget * col + (1.0 - forget) * lax.optimization_barrier(jnp.mean(square, axis=-2))
    row_mean = lax.optimization_barrier(jnp.mean(row_new, axis=-1))
    vhat = row_new[..., :, None] * col_new[..., None, :] / row_mean[..., None, None]
    raw = grad / jnp.sqrt(vhat)
    clip_factor = jnp.maximum(1.0, jnp.sqrt(lax.optimization_barrier(jnp.mean(raw * raw, axis=(-2, -1)))))
    step_size = relative * jnp.sqrt(lax.optimization_barrier(jnp.mean(param * param, axis=(-2, -1))))
    update = -(step_size / clip_factor)[..., None, None] * raw
    updated = param + update
    return (updated, update, row_new, col_new)

def reference(tokens, inner_weight, inner_grad, inner_row, inner_col, outer_weight, outer_grad, outer_row, outer_col):
    inner_new, inner_update, inner_row_new, inner_col_new = factor_update(inner_weight, inner_grad, inner_row, inner_col)
    outer_new, outer_update, outer_row_new, outer_col_new = factor_update(outer_weight, outer_grad, outer_row, outer_col)
    inner_cast = inner_new.astype(jnp.bfloat16)
    gate_pre = jnp.dot(tokens, inner_cast[0], preferred_element_type=jnp.float32)
    up_pre = jnp.dot(tokens, inner_cast[1], preferred_element_type=jnp.float32)
    hidden = (jax.nn.gelu(gate_pre, approximate=True) * up_pre).astype(jnp.bfloat16)
    return (inner_new, inner_update, inner_row_new, inner_col_new, outer_new, outer_update, outer_row_new, outer_col_new, hidden)
```

```python
import functools

import jax
import jax.numpy as jnp
from jax import lax
from jax.experimental import pallas as pl
from jax.experimental.pallas import tpu as pltpu
from jax.sharding import PartitionSpec as P

D = 4096
FF = 16384
STEP = 10
FORGET = 1.0 - STEP ** (-0.8)
FRESH = 1.0 - FORGET
RELATIVE = min(0.01, STEP ** (-0.5))


def partners(count, flip):
    return [(i, i ^ flip) for i in range(count)]


def swap(x, axis, flip):
    return lax.ppermute(x, axis, partners(lax.axis_size(axis), flip))


def total(x, axis, radix):
    count, base = lax.axis_size(axis), 1
    for width in radix:
        width = min(width, count // base)
        if width < 2:
            break
        terms = [x] + [swap(x, axis, base * k) for k in range(1, width)]
        while len(terms) > 1:
            terms = [terms[i] + terms[i + 1] for i in range(0, len(terms), 2)]
        x, base = terms[0], base * width
    assert base == count
    return x


def rounds(axis, first):
    count, out = lax.axis_size(axis), []
    left = count
    for width in (*first, *[4] * 8):
        if left > 1:
            width = min(width, left)
            out.append(width)
            left //= width
    return out


def tie(x, *after):
    return lax.optimization_barrier((x, *after))[0]


def bits_of(count):
    return [1 << i for i in range(count.bit_length() - 1)]


def update_kernel(picks, coef, x_ref, row_ref, col_ref, grad_ref, weight_ref, *refs):
    new_ref, update_ref, send_ref, keep_ref, cast_ref = refs[-5:]
    group = pl.program_id(0)
    width = grad_ref.shape[2]
    scale = coef[group]
    row = row_ref[0]
    for lane in range(0, width, 128):
        at = slice(lane, lane + 128)
        update = grad_ref[0, :, at] * row * (col_ref[0, :, at] * scale)
        new = weight_ref[0, :, at] + update
        update_ref[0, :, at] = update
        new_ref[0, :, at] = new
        cast_ref[:, at] = new.astype(jnp.bfloat16)
    product = jnp.dot(x_ref[...], cast_ref[...], preferred_element_type=jnp.float32)
    send, keep, rows = picks
    for place, block in enumerate(send):
        send_ref[0, place] = product[block * rows : (block + 1) * rows].astype(jnp.bfloat16)
    for place, block in enumerate(keep):
        keep_ref[0, place] = product[block * rows : (block + 1) * rows]


def update_chunk(coef, x, row, col, grad, weight, held, start, width, send, keep):
    groups, depth, columns = grad.shape
    rows = x.shape[0] // (len(send) + len(keep))
    step = min(256, width)
    first = start // step
    cols = lambda g, j: (g, 0, first + j)
    whole = pl.BlockSpec((1, depth, step), cols)
    part = lambda count: pl.BlockSpec((1, count, rows, step), lambda g, j: (g, 0, 0, j))
    big = jax.ShapeDtypeStruct(grad.shape, jnp.float32)
    extra = [] if held is None else list(held)
    return pl.pallas_call(
        functools.partial(update_kernel, (send, keep, rows)),
        grid=(groups, width // step),
        in_specs=[
            pl.BlockSpec(memory_space=pltpu.SMEM),
            pl.BlockSpec(x.shape, lambda g, j: (0, 0)),
            pl.BlockSpec((1, depth, 128), lambda g, j: (g, 0, 0)),
            pl.BlockSpec((1, 1, step), cols),
            whole,
            whole,
            *[pl.BlockSpec(memory_space=pl.ANY) for _ in extra],
        ],
        out_specs=[whole, whole, part(len(send)), part(len(keep))],
        out_shape=[
            big,
            big,
            jax.ShapeDtypeStruct((groups, len(send), rows, width), jnp.bfloat16),
            jax.ShapeDtypeStruct((groups, len(keep), rows, width), jnp.float32),
        ],
        scratch_shapes=[pltpu.VMEM((depth, step), jnp.bfloat16)],
        input_output_aliases={6: 0, 7: 1} if extra else {},
        cost_estimate=pl.CostEstimate(
            flops=2 * x.shape[0] * depth * width * groups,
            bytes_accessed=groups * width * (16 * depth + 3 * x.shape[0]),
            transcendentals=0,
        ),
        name="update_chunk",
    )(coef, x, row, col, grad, weight, *extra)


def plan(columns, count):
    bits = bits_of(count)
    pieces = min(4, columns // 128)
    width = columns // pieces
    return [(i * width, width, bits[i % len(bits) :] + bits[: i % len(bits)]) for i in range(pieces)]


def split(blocks, bit):
    return [b for b in blocks if b & bit], [b for b in blocks if not b & bit]


def per_device(
    tokens, inner_weight, inner_grad, inner_row, inner_col, outer_weight, outer_grad, outer_row, outer_col
):
    data_count, model_count = lax.axis_size("dp"), lax.axis_size("mp")
    data_index, model_index = lax.axis_index("dp"), lax.axis_index("mp")
    groups, depth, columns = inner_grad.shape
    rows = tokens.shape[0]
    half = rows // 2
    core = model_index % 2
    sum_data = lambda v: total(v, "dp", rounds("dp", (4,)))
    sum_model = lambda v: total(v, "mp", rounds("mp", (2,)))

    col_sum = sum_data(jnp.sum(inner_grad * inner_grad + 1e-30, axis=1))
    inner_col_new = FORGET * inner_col + FRESH * (col_sum / D)
    inverse_col = 1.0 / inner_col_new

    tokens_late = tie(tokens, col_sum)
    mine = []
    for flip in range(data_count):
        start = (core * half, (data_index ^ flip) * depth)
        piece = lax.dynamic_slice(tokens_late, start, (half, depth))
        mine.append(piece if flip == 0 else swap(piece, "dp", flip))
    mine = jnp.stack(mine)
    theirs = swap(mine, "mp", 1)
    x = jnp.where(core == 0, jnp.stack([mine, theirs], 1), jnp.stack([theirs, mine], 1))
    x = x.reshape(data_count * rows, depth)

    weight_sq = jnp.sum(inner_weight * inner_weight, axis=(1, 2))
    inner_sq = inner_grad * inner_grad
    row_sum = jnp.sum(inner_sq + 1e-30, axis=2)
    weighted = jnp.sum(inner_sq * inverse_col[:, None, :], axis=2)
    packed = jnp.concatenate([row_sum, weighted, jnp.broadcast_to(weight_sq[:, None], (groups, 128))], 1)
    packed = sum_model(packed)
    row_sum, weighted, weight_sq = packed[:, :depth], packed[:, depth : 2 * depth], packed[:, 2 * depth]
    inner_row_new = FORGET * inner_row + FRESH * (row_sum / FF)
    scalars = jnp.stack([jnp.sum(inner_row_new, 1), jnp.sum(weighted / inner_row_new, 1), weight_sq], 1)
    scalars = sum_data(jnp.broadcast_to(scalars[:, :, None], (groups, 3, 128)))[:, :, 0]
    mean = scalars[:, 0] / D
    clip = jnp.maximum(1.0, jnp.sqrt(mean * scalars[:, 1] / (D * FF)))
    step = RELATIVE * jnp.sqrt(scalars[:, 2] / (D * FF))
    coef = -(step / clip) * jnp.sqrt(mean)
    row = jnp.broadcast_to(lax.rsqrt(inner_row_new)[:, :, None], (groups, depth, 128))
    col = lax.rsqrt(inner_col_new)[:, None, :]

    held, chunks = None, []
    for start, width, order in plan(columns, data_count):
        blocks = list(range(data_count))
        send, keep = split(blocks, order[0])
        new, update, sent, kept = update_chunk(
            coef, x, row, col, inner_grad, inner_weight, held, start, width, send, keep
        )
        held = (new, update)
        chunks.append((keep, order, swap(sent, "dp", order[0]), kept))
    inner_new, inner_update = held

    for level in range(1, len(bits_of(data_count))):
        later = []
        for blocks, order, came, kept in chunks:
            send, keep = split(blocks, order[level])
            pick = lambda which: [blocks.index(b) for b in which]
            take = lambda v, which: jnp.stack([v[:, i].astype(jnp.float32) for i in pick(which)], 1)
            sent = (take(kept, send) + take(came, send)).astype(jnp.bfloat16)
            later.append((keep, order, swap(sent, "dp", order[level]), take(kept, keep) + take(came, keep)))
        chunks = later
    pieces = []
    for _, _, came, kept in chunks:
        both = kept[:, 0] + came[:, 0].astype(jnp.float32)
        pieces.append((jax.nn.gelu(both[0], approximate=True) * both[1]).astype(jnp.bfloat16))
    hidden = jnp.concatenate(pieces, 1)

    outer_sq = outer_grad * outer_grad
    outer_row_sum = sum_data(jnp.sum(outer_sq + 1e-30, axis=1))
    outer_row_new = FORGET * outer_row + FRESH * (outer_row_sum / D)
    outer_weight_sq = jnp.sum(outer_weight * outer_weight)
    col_sum = jnp.sum(outer_sq + 1e-30, axis=0)
    weighted = jnp.sum(outer_sq * (1.0 / outer_row_new)[:, None], axis=0)
    packed = jnp.concatenate([col_sum, weighted, jnp.broadcast_to(outer_weight_sq, (128,)), jnp.broadcast_to(jnp.sum(outer_row_new), (128,))])
    packed = sum_model(packed)
    width = outer_col.shape[0]
    outer_col_new = FORGET * outer_col + FRESH * (packed[:width] / FF)
    scalars = jnp.stack([jnp.sum(packed[width : 2 * width] / outer_col_new), packed[2 * width]])
    scalars = sum_data(jnp.broadcast_to(scalars[:, None], (2, 128)))[:, 0]
    mean = packed[2 * width + 128] / FF
    clip = jnp.maximum(1.0, jnp.sqrt(mean * scalars[0] / (D * FF)))
    step = RELATIVE * jnp.sqrt(scalars[1] / (D * FF))
    scale = -(step / clip) * jnp.sqrt(mean)
    outer_update = outer_grad * (lax.rsqrt(outer_row_new)[:, None] * (lax.rsqrt(outer_col_new) * scale)[None, :])
    outer_new = outer_weight + outer_update
    return (
        inner_new,
        inner_update,
        inner_row_new,
        inner_col_new,
        outer_new,
        outer_update,
        outer_row_new,
        outer_col_new,
        hidden,
    )


def solution(mesh):
    placed = (
        P("dp", None),
        P(None, "dp", "mp"),
        P(None, "dp", "mp"),
        P(None, "dp"),
        P(None, "mp"),
        P("mp", "dp"),
        P("mp", "dp"),
        P("mp"),
        P("dp"),
    )
    return jax.shard_map(
        per_device,
        mesh=mesh,
        in_specs=placed,
        out_specs=(
            P(None, "dp", "mp"),
            P(None, "dp", "mp"),
            P(None, "dp"),
            P(None, "mp"),
            P("mp", "dp"),
            P("mp", "dp"),
            P("mp"),
            P("dp"),
            P("dp", "mp"),
        ),
        check_vma=False,
    )
```

```python
import functools

import jax
import jax.numpy as jnp
from jax import lax
from jax.experimental import pallas as pl
from jax.experimental.pallas import tpu as pltpu
from jax.sharding import PartitionSpec as P


D = 4096
FF = 16384
STEP = 10
FORGET = 1.0 - STEP ** (-0.8)
FRESH = 1.0 - FORGET
RELATIVE = min(0.01, STEP ** (-0.5))
LIMIT = 24 << 20


def partners(count, flip):
    return [(i, i ^ flip) for i in range(count)]


def swap(x, axis, flip):
    return lax.ppermute(x, axis, partners(lax.axis_size(axis), flip))


def total(x, axis, radix):
    count, base = lax.axis_size(axis), 1
    for width in radix:
        width = min(width, count // base)
        if width < 2:
            break
        terms = [x] + [swap(x, axis, base * k) for k in range(1, width)]
        while len(terms) > 1:
            terms = [terms[i] + terms[i + 1] for i in range(0, len(terms), 2)]
        x, base = terms[0], base * width
    assert base == count
    return x


def rounds(axis, first):
    count, out = lax.axis_size(axis), []
    left = count
    for width in (*first, *[4] * 8):
        if left > 1:
            width = min(width, left)
            out.append(width)
            left //= width
    return out


def tie(x, *after):
    return lax.optimization_barrier((x, *after))[0]


def bits_of(count):
    return [1 << i for i in range(count.bit_length() - 1)]


def far(x):
    return pltpu.with_memory_space_constraint(x, pltpu.HBM)


WHOLE = pl.BlockSpec(memory_space=pltpu.VMEM)
LEFT = pl.BlockSpec(memory_space=pl.ANY)


def tree(values):
    while len(values) > 1:
        pairs = [values[i] + values[i + 1] for i in range(0, len(values) - 1, 2)]
        values = pairs + values[len(values) - len(values) % 2 :]
    return values[0]


def fetch(source, held, sems, blocks, start=True):
    groups, depth = held.shape[:2]
    height = depth // blocks
    copies = []
    for group in range(groups):
        for block in range(blocks):
            at = (group, pl.ds(block * height, height))
            copies.append(pltpu.make_async_copy(source.at[at], held.at[at], sems.at[group * blocks + block]))
    for copy in copies if start else ():
        copy.start()
    return copies, height


def col_kernel(blocks, grad_ref, sum_ref, held, sems):
    groups, depth, columns = held.shape
    copies, height = fetch(grad_ref, held, sems, blocks)
    for group in range(groups):
        sums = jnp.zeros((8, columns), jnp.float32)
        for block in range(blocks):
            copies[group * blocks + block].wait()

            def add(i, sums):
                value = held[group, pl.ds(pl.multiple_of(block * height + i * 8, 8), 8), :]
                return sums + value * value

            sums = lax.fori_loop(0, height // 8, add, sums, unroll=4)
        sum_ref[group : group + 1, :] = jnp.sum(sums, axis=0, keepdims=True) + depth * 1e-30


def row_kernel(blocks, grad_ref, weight_ref, inverse_ref, packed_ref, held, weights, plain_ref, over_ref, sems, more):
    groups, depth, columns = held.shape
    copies, height = fetch(grad_ref, held, sems, blocks, False)
    weight_copies, _ = fetch(weight_ref, weights, more, blocks, False)
    for pair in zip(copies, weight_copies):
        for copy in pair:
            copy.start()
    ones = jnp.ones((8, 128), jnp.float32)
    across = lambda v: lax.dot_general(
        ones, v, (((1,), (1,)), ((), ())), precision=lax.Precision.HIGHEST, preferred_element_type=jnp.float32
    )
    for group in range(groups):
        inverse = jnp.broadcast_to(inverse_ref[group : group + 1, :], (8, columns))
        sums = jnp.zeros((8, columns), jnp.float32)
        for block in range(blocks):
            copies[group * blocks + block].wait()

            @pl.loop(0, height // 8, unroll=2)
            def _(i):
                at = pl.ds(pl.multiple_of(block * height + i * 8, 8), 8)
                lanes = [slice(lane, lane + 128) for lane in range(0, columns, 128)]
                squares = [held[group, at, lane] * held[group, at, lane] for lane in lanes]
                plain_ref[at, :] = tree(squares)
                over_ref[at, :] = tree([square * inverse[:, lane] for square, lane in zip(squares, lanes)])

            weight_copies[group * blocks + block].wait()

            def add(i, sums):
                value = weights[group, pl.ds(pl.multiple_of(block * height + i * 8, 8), 8), :]
                return sums + value * value

            sums = lax.fori_loop(0, height // 8, add, sums, unroll=4)
        packed_ref[group : group + 1, :depth] = across(plain_ref[...])[:1] + columns * 1e-30
        packed_ref[group : group + 1, depth : 2 * depth] = across(over_ref[...])[:1]
        packed_ref[group : group + 1, 2 * depth :] = jnp.full((1, 128), jnp.sum(sums), jnp.float32)


def statistics(kernel, bigs, small, out, more):
    big = bigs[0]
    groups, depth, _ = big.shape
    blocks = min(8, depth // 8)
    sems = pltpu.SemaphoreType.DMA((groups * blocks,))
    return pl.pallas_call(
        functools.partial(kernel, blocks),
        in_specs=[LEFT] * len(bigs) + [WHOLE] * len(small),
        out_specs=WHOLE,
        out_shape=jax.ShapeDtypeStruct(out, jnp.float32),
        scratch_shapes=[*[pltpu.VMEM(v.shape, jnp.float32) for v in bigs], *more, *[sems for _ in bigs]],
        compiler_params=pltpu.CompilerParams(vmem_limit_bytes=(6 << 20) + sum(4 * v.size for v in bigs)),
        cost_estimate=pl.CostEstimate(
            flops=4 * big.size * len(bigs), bytes_accessed=4 * big.size * len(bigs), transcendentals=0
        ),
    )(*map(far, bigs), *small)


def update_kernel(picks, coef, row_ref, col_ref, grad_ref, weight_ref, *refs):
    new_ref, update_ref, send_ref, keep_ref, cast_ref = refs[-5:]
    group = pl.program_id(0)
    width = grad_ref.shape[2]
    scale = coef[group]
    row = row_ref[0]
    for lane in range(0, width, 128):
        at = slice(lane, lane + 128)
        update = grad_ref[0, :, at] * row * (col_ref[0, :, at] * scale)
        new = weight_ref[0, :, at] + update
        update_ref[0, :, at] = update
        new_ref[0, :, at] = new
        cast_ref[:, at] = new.astype(jnp.bfloat16)
    send, keep = picks
    for ref, blocks in ((send_ref, send), (keep_ref, keep)):
        for place, block in enumerate(blocks):
            product = jnp.dot(refs[block][...], cast_ref[...], preferred_element_type=jnp.float32)
            ref[0, place] = product.astype(ref.dtype)


def update_chunk(coef, tokens, row, col, grad, weight, held, start, width, send, keep):
    groups, depth, _ = grad.shape
    count = len(send) + len(keep)
    rows = tokens[0].shape[0]
    step = min(512, width)
    first = start // step
    cols = lambda g, j: (g, 0, first + j)
    whole = pl.BlockSpec((1, depth, step), cols)
    part = lambda count: pl.BlockSpec((1, count, rows, step), lambda g, j: (g, 0, 0, j))
    out = lambda count: pltpu.HBM((groups, count, rows, width), jnp.bfloat16)
    big = jax.ShapeDtypeStruct(grad.shape, jnp.float32)
    extra = [] if held is None else list(held)
    return pl.pallas_call(
        functools.partial(update_kernel, (send, keep)),
        grid=(groups, width // step),
        in_specs=[
            pl.BlockSpec(memory_space=pltpu.SMEM),
            pl.BlockSpec((1, depth, 128), lambda g, j: (g, 0, 0)),
            pl.BlockSpec((1, 1, step), cols),
            whole,
            whole,
            *[pl.BlockSpec(piece.shape, lambda g, j: (0, 0)) for piece in tokens],
            *[LEFT for _ in extra],
        ],
        out_specs=[whole, whole, part(len(send)), part(len(keep))],
        out_shape=[big, big, out(len(send)), out(len(keep))],
        scratch_shapes=[pltpu.VMEM((depth, step), jnp.bfloat16)],
        input_output_aliases={5 + count: 0, 6 + count: 1} if extra else {},
        compiler_params=pltpu.CompilerParams(vmem_limit_bytes=LIMIT),
        cost_estimate=pl.CostEstimate(
            flops=2 * count * rows * depth * width * groups,
            bytes_accessed=groups * width * (16 * depth + 2 * count * rows),
            transcendentals=0,
        ),
        name="update_chunk",
    )(coef, row, col, far(grad), far(weight), *tokens, *extra)


def spread_kernel(factor_ref, row_ref):
    groups, depth = factor_ref.shape
    for group in range(groups):
        for start in range(0, depth, 128):
            factor = lax.rsqrt(factor_ref[group : group + 1, start : start + 128])
            row_ref[group, start : start + 128, :] = jnp.broadcast_to(factor, (128, 128)).T


def spread_rows(factor):
    shape = (*factor.shape, 128)
    return pl.pallas_call(
        spread_kernel,
        in_specs=[WHOLE],
        out_specs=WHOLE,
        out_shape=jax.ShapeDtypeStruct(shape, jnp.float32),
        compiler_params=pltpu.CompilerParams(vmem_limit_bytes=LIMIT),
        cost_estimate=pl.CostEstimate(flops=0, bytes_accessed=512 * factor.size, transcendentals=0),
        name="spread_rows",
    )(factor)


def combine_kernel(count, *refs):
    refs[-1][...] = sum(ref[...].astype(jnp.float32) for ref in refs[:count]).astype(jnp.bfloat16)


def combine(terms, blocks):
    groups, _, rows, width = terms[0][0].shape

    def pick(names):
        places = [names.index(block) for block in blocks]
        place = lambda b: functools.reduce(lambda rest, i: jnp.where(b == i, places[i], rest), range(1, len(places)), places[0])
        return pl.BlockSpec((1, 1, rows, width), lambda g, b: (g, place(b), 0, 0))

    return pl.pallas_call(
        functools.partial(combine_kernel, len(terms)),
        grid=(groups, len(blocks)),
        in_specs=[pick(names) for _, names in terms],
        out_specs=pl.BlockSpec((1, 1, rows, width), lambda g, b: (g, b, 0, 0)),
        out_shape=jax.ShapeDtypeStruct((groups, len(blocks), rows, width), jnp.bfloat16),
        compiler_params=pltpu.CompilerParams(vmem_limit_bytes=LIMIT),
        cost_estimate=pl.CostEstimate(
            flops=0, bytes_accessed=2 * (len(terms) + 1) * groups * len(blocks) * rows * width, transcendentals=0
        ),
        name="combine",
    )(*[value for value, _ in terms])


def final_kernel(counts, *refs):
    out_ref, place, start = refs[-1], 0, 0
    for count in counts:
        terms = refs[place : place + count]
        gate, up = [sum(ref[g, 0].astype(jnp.float32) for ref in terms) for g in range(2)]
        width = gate.shape[1]
        out_ref[:, start : start + width] = (jax.nn.gelu(gate, approximate=True) * up).astype(out_ref.dtype)
        place, start = place + count, start + width


def finish(chunks):
    rows = chunks[0][0][0].shape[2]
    columns = sum(terms[0][0].shape[3] for terms in chunks)
    height = rows // 4
    terms = [term for chunk in chunks for term in chunk]
    spec = lambda value, place: pl.BlockSpec((2, 1, height, value.shape[3]), lambda i: (0, place, i, 0))
    return pl.pallas_call(
        functools.partial(final_kernel, [len(chunk) for chunk in chunks]),
        grid=(rows // height,),
        in_specs=[spec(value, place) for value, place in terms],
        out_specs=pl.BlockSpec((height, columns), lambda i: (i, 0)),
        out_shape=jax.ShapeDtypeStruct((rows, columns), jnp.bfloat16),
        compiler_params=pltpu.CompilerParams(vmem_limit_bytes=LIMIT),
        cost_estimate=pl.CostEstimate(
            flops=0, bytes_accessed=20 * rows * columns, transcendentals=rows * columns
        ),
        name="finish",
    )(*[value for value, _ in terms])


def plan(columns, count):
    bits = bits_of(count)
    pieces = min(4, columns // 128)
    width = columns // pieces
    return [
        (i * width, width, bits[i % len(bits) :] + bits[: i % len(bits)]) for i in range(pieces)
    ]


def split(blocks, bit):
    return [b for b in blocks if b & bit], [b for b in blocks if not b & bit]


def program(
    tokens, inner_weight, inner_grad, inner_row, inner_col, outer_weight, outer_grad, outer_row, outer_col
):
    data_count = lax.axis_size("dp")
    data_index = lax.axis_index("dp")
    groups, depth, columns = inner_grad.shape
    sum_data = lambda v: total(v, "dp", rounds("dp", (4,)))
    sum_model = lambda v: total(v, "mp", rounds("mp", (2,)))

    col_part = statistics(col_kernel, (inner_grad,), (), (groups, columns), ())
    col_sum = sum_data(col_part)
    inner_col_new = FORGET * inner_col + FRESH * (col_sum / D)
    inverse_col = 1.0 / inner_col_new
    tokens_late = tie(tokens, col_part)
    share = []
    for flip in range(data_count):
        piece = lax.dynamic_slice_in_dim(tokens_late, (data_index ^ flip) * depth, depth, 1)
        share.append(piece if flip == 0 else swap(piece, "dp", flip))

    columned = [pltpu.VMEM((depth, 128), jnp.float32)] * 2
    packed = statistics(row_kernel, (inner_grad, inner_weight), (inverse_col,), (groups, 2 * depth + 128), columned)
    outer_grad = tie(outer_grad, packed)
    outer_sq = outer_grad * outer_grad
    outer_part = jnp.sum(outer_sq + 1e-30, axis=1)
    outer_weight = tie(outer_weight, packed)
    outer_weight_sq = jnp.sum(outer_weight * outer_weight)
    packed = sum_model(packed)
    row_sum, weighted, weight_sq = packed[:, :depth], packed[:, depth : 2 * depth], packed[:, 2 * depth]
    inner_row_new = FORGET * inner_row + FRESH * (row_sum / FF)
    scalars = jnp.stack([jnp.sum(inner_row_new, 1), jnp.sum(weighted / inner_row_new, 1), weight_sq], 1)
    scalars = jnp.broadcast_to(scalars[:, :, None], (groups, 3, 128)).reshape(-1)
    scalars = sum_data(jnp.concatenate([outer_part, scalars]))
    outer_row_sum = scalars[: outer_part.size]
    scalars = scalars[outer_part.size :].reshape(groups, 3, 128)[:, :, 0]
    mean = scalars[:, 0] / D
    clip = jnp.maximum(1.0, jnp.sqrt(mean * scalars[:, 1] / (D * FF)))
    step = RELATIVE * jnp.sqrt(scalars[:, 2] / (D * FF))
    coef = -(step / clip) * jnp.sqrt(mean)
    row = spread_rows(inner_row_new)
    col = lax.rsqrt(inner_col_new)[:, None, :]

    held, chunks = None, []
    for start, width, order in plan(columns, data_count):
        send, keep = split(list(range(data_count)), order[0])
        *held, sent, kept = update_chunk(
            coef, share, row, col, inner_grad, inner_weight, held, start, width, send, keep
        )
        came = swap(sent, "dp", order[0])
        chunks.append((start, width, order, keep, [(kept, keep), (came, keep)]))
    inner_new, inner_update = held

    for level in range(1, len(bits_of(data_count))):
        later = []
        for start, width, order, blocks, terms in chunks:
            send, keep = split(blocks, order[level])
            sent = combine(terms, send)
            came = swap(sent, "dp", order[level])
            later.append((start, width, order, keep, [*terms, (came, keep)]))
        chunks = later
    hidden = finish([[(value, names.index(0)) for value, names in terms] for *_, terms in chunks])

    outer_row_new = FORGET * outer_row + FRESH * (outer_row_sum / D)
    outer_grad = tie(outer_grad, outer_row_new)
    outer_sq = outer_grad * outer_grad
    col_sum = jnp.sum(outer_sq + 1e-30, axis=0)
    weighted = jnp.sum(outer_sq * (1.0 / outer_row_new)[:, None], axis=0)
    spare = jnp.broadcast_to(jnp.stack([outer_weight_sq, jnp.sum(outer_row_new)])[:, None], (2, 128)).reshape(-1)
    packed = jnp.concatenate([col_sum, weighted, spare])
    packed = sum_model(packed)
    width = outer_col.shape[0]
    outer_col_new = FORGET * outer_col + FRESH * (packed[:width] / FF)
    scalars = jnp.stack([jnp.sum(packed[width : 2 * width] / outer_col_new), packed[2 * width]])
    scalars = sum_data(jnp.broadcast_to(scalars[:, None], (2, 128)))[:, 0]
    mean = packed[2 * width + 128] / FF
    clip = jnp.maximum(1.0, jnp.sqrt(mean * scalars[0] / (D * FF)))
    step = RELATIVE * jnp.sqrt(scalars[1] / (D * FF))
    scale = -(step / clip) * jnp.sqrt(mean)
    outer_update = outer_grad * (lax.rsqrt(outer_row_new)[:, None] * (lax.rsqrt(outer_col_new) * scale)[None, :])
    outer_new = outer_weight + outer_update
    return (
        inner_new,
        inner_update,
        inner_row_new,
        inner_col_new,
        outer_new,
        outer_update,
        outer_row_new,
        outer_col_new,
        hidden,
    )


def solution(mesh):
    placed = (
        P("dp", None),
        P(None, "dp", "mp"),
        P(None, "dp", "mp"),
        P(None, "dp"),
        P(None, "mp"),
        P("mp", "dp"),
        P("mp", "dp"),
        P("mp"),
        P("dp"),
    )
    return jax.shard_map(
        program,
        mesh=mesh,
        in_specs=placed,
        out_specs=(
            P(None, "dp", "mp"),
            P(None, "dp", "mp"),
            P(None, "dp"),
            P(None, "mp"),
            P("mp", "dp"),
            P("mp", "dp"),
            P("mp"),
            P("dp"),
            P("dp", "mp"),
        ),
        check_vma=False,
    )
```

```python
import functools

import jax
import jax.numpy as jnp
from jax import lax
from jax.experimental import pallas as pl
from jax.experimental.pallas import tpu as pltpu
from jax.sharding import PartitionSpec as P


D = 4096
FF = 16384
STEP = 10
FORGET = 1.0 - STEP ** (-0.8)
FRESH = 1.0 - FORGET
RELATIVE = min(0.01, STEP ** (-0.5))
LIMIT = 24 << 20


def partners(count, flip):
    return [(i, i ^ flip) for i in range(count)]


def swap(x, axis, flip):
    return lax.ppermute(x, axis, partners(lax.axis_size(axis), flip))


def total(x, axis, radix):
    count, base = lax.axis_size(axis), 1
    for width in radix:
        width = min(width, count // base)
        if width < 2:
            break
        terms = [x] + [swap(x, axis, base * k) for k in range(1, width)]
        while len(terms) > 1:
            terms = [terms[i] + terms[i + 1] for i in range(0, len(terms), 2)]
        x, base = terms[0], base * width
    assert base == count
    return x


def rounds(axis, first):
    count, out = lax.axis_size(axis), []
    left = count
    for width in (*first, *[4] * 8):
        if left > 1:
            width = min(width, left)
            out.append(width)
            left //= width
    return out


def tie(x, *after):
    return lax.optimization_barrier((x, *after))[0]


def bits_of(count):
    return [1 << i for i in range(count.bit_length() - 1)]


def far(x):
    return pltpu.with_memory_space_constraint(x, pltpu.HBM)


WHOLE = pl.BlockSpec(memory_space=pltpu.VMEM)
LEFT = pl.BlockSpec(memory_space=pl.ANY)


def tree(values):
    while len(values) > 1:
        pairs = [values[i] + values[i + 1] for i in range(0, len(values) - 1, 2)]
        values = pairs + values[len(values) - len(values) % 2 :]
    return values[0]


def fetch(source, held, sems, blocks, start=True):
    groups, depth = held.shape[:2]
    height = depth // blocks
    copies = []
    for group in range(groups):
        for block in range(blocks):
            at = (group, pl.ds(block * height, height))
            copies.append(pltpu.make_async_copy(source.at[at], held.at[at], sems.at[group * blocks + block]))
    for copy in copies if start else ():
        copy.start()
    return copies, height


def col_kernel(floor, blocks, grad_ref, sum_ref, held, sems):
    groups, depth, columns = held.shape
    copies, height = fetch(grad_ref, held, sems, blocks)
    for group in range(groups):
        sums = jnp.zeros((8, columns), jnp.float32)
        for block in range(blocks):
            copies[group * blocks + block].wait()

            def add(i, sums):
                value = held[group, pl.ds(pl.multiple_of(block * height + i * 8, 8), 8), :]
                return sums + value * value

            sums = lax.fori_loop(0, height // 8, add, sums, unroll=4)
        sum_ref[group : group + 1, :] = jnp.sum(sums, axis=0, keepdims=True) + depth * floor


def row_kernel(blocks, grad_ref, weight_ref, inverse_ref, packed_ref, held, weights, plain_ref, over_ref, sems, more):
    groups, depth, columns = held.shape
    copies, height = fetch(grad_ref, held, sems, blocks, False)
    weight_copies, _ = fetch(weight_ref, weights, more, blocks, False)
    for pair in zip(copies, weight_copies):
        for copy in pair:
            copy.start()
    ones = jnp.ones((8, 128), jnp.float32)
    across = lambda v: lax.dot_general(
        ones, v, (((1,), (1,)), ((), ())), precision=lax.Precision.HIGHEST, preferred_element_type=jnp.float32
    )
    for group in range(groups):
        inverse = jnp.broadcast_to(inverse_ref[group : group + 1, :], (8, columns))
        sums = jnp.zeros((8, columns), jnp.float32)
        for block in range(blocks):
            copies[group * blocks + block].wait()

            @pl.loop(0, height // 8, unroll=2)
            def _(i):
                at = pl.ds(pl.multiple_of(block * height + i * 8, 8), 8)
                lanes = [slice(lane, lane + 128) for lane in range(0, columns, 128)]
                squares = [held[group, at, lane] * held[group, at, lane] for lane in lanes]
                plain_ref[at, :] = tree(squares)
                over_ref[at, :] = tree([square * inverse[:, lane] for square, lane in zip(squares, lanes)])

            weight_copies[group * blocks + block].wait()

            def add(i, sums):
                value = weights[group, pl.ds(pl.multiple_of(block * height + i * 8, 8), 8), :]
                return sums + value * value

            sums = lax.fori_loop(0, height // 8, add, sums, unroll=4)
        packed_ref[group : group + 1, :depth] = across(plain_ref[...])[:1] + columns * 1e-30
        packed_ref[group : group + 1, depth : 2 * depth] = across(over_ref[...])[:1]
        packed_ref[group : group + 1, 2 * depth :] = jnp.full((1, 128), jnp.sum(sums), jnp.float32)


def outer_kernel(blocks, grad_ref, weight_ref, row_ref, packed_ref, held, weights, spread, sems, more):
    _, depth, columns = held.shape
    copies, height = fetch(grad_ref, held, sems, blocks, False)
    weight_copies, _ = fetch(weight_ref, weights, more, blocks, False)
    for pair in zip(copies, weight_copies):
        for copy in pair:
            copy.start()
    for start in range(0, depth, 128):
        factor = 1.0 / row_ref[:, start : start + 128]
        spread[start : start + 128, :] = jnp.broadcast_to(factor, (128, 128)).T
    sums = (jnp.zeros((8, columns), jnp.float32),) * 3
    for block in range(blocks):
        copies[block].wait()
        weight_copies[block].wait()

        def add(i, sums):
            at = pl.ds(pl.multiple_of(block * height + i * 8, 8), 8)
            square = held[0, at, :] * held[0, at, :]
            weight = weights[0, at, :]
            over = square * jnp.concatenate([spread[at, :]] * (columns // 128), axis=1)
            return sums[0] + square, sums[1] + over, sums[2] + weight * weight

        sums = lax.fori_loop(0, height // 8, add, sums, unroll=4)
    packed_ref[:, :columns] = jnp.sum(sums[0], axis=0, keepdims=True) + depth * 1e-30
    packed_ref[:, columns : 2 * columns] = jnp.sum(sums[1], axis=0, keepdims=True)
    packed_ref[:, 2 * columns : 2 * columns + 128] = jnp.full((1, 128), jnp.sum(sums[2]), jnp.float32)
    packed_ref[:, 2 * columns + 128 :] = jnp.full((1, 128), jnp.sum(row_ref[...]), jnp.float32)


def statistics(kernel, bigs, small, out, more):
    big = bigs[0]
    groups, depth, _ = big.shape
    blocks = min(8, depth // 8)
    sems = pltpu.SemaphoreType.DMA((groups * blocks,))
    return pl.pallas_call(
        functools.partial(kernel, blocks),
        in_specs=[LEFT] * len(bigs) + [WHOLE] * len(small),
        out_specs=WHOLE,
        out_shape=jax.ShapeDtypeStruct(out, jnp.float32),
        scratch_shapes=[*[pltpu.VMEM(v.shape, jnp.float32) for v in bigs], *more, *[sems for _ in bigs]],
        compiler_params=pltpu.CompilerParams(vmem_limit_bytes=(6 << 20) + sum(4 * v.size for v in bigs)),
        cost_estimate=pl.CostEstimate(
            flops=4 * big.size * len(bigs), bytes_accessed=4 * big.size * len(bigs), transcendentals=0
        ),
    )(*map(far, bigs), *small)


def update_kernel(picks, coef, row_ref, col_ref, grad_ref, weight_ref, *refs):
    new_ref, update_ref, send_ref, keep_ref, cast_ref = refs[-5:]
    group = pl.program_id(0)
    width = grad_ref.shape[2]
    scale = coef[group]
    row = row_ref[0]
    for lane in range(0, width, 128):
        at = slice(lane, lane + 128)
        update = grad_ref[0, :, at] * row * (col_ref[0, :, at] * scale)
        new = weight_ref[0, :, at] + update
        update_ref[0, :, at] = update
        new_ref[0, :, at] = new
        cast_ref[:, at] = new.astype(jnp.bfloat16)
    send, keep = picks
    for ref, blocks in ((send_ref, send), (keep_ref, keep)):
        for place, block in enumerate(blocks):
            product = jnp.dot(refs[block][...], cast_ref[...], preferred_element_type=jnp.float32)
            ref[0, place] = product.astype(ref.dtype)


def update_chunk(coef, tokens, row, col, grad, weight, held, start, width, send, keep):
    groups, depth, _ = grad.shape
    count = len(send) + len(keep)
    rows = tokens[0].shape[0]
    cols = lambda g: (g, 0, start)
    whole = pl.BlockSpec((pl.Element(1), pl.Element(depth), pl.Element(width)), cols)
    part = lambda count: pl.BlockSpec((1, count, rows, width), lambda g: (g, 0, 0, 0))
    out = lambda count: pltpu.HBM((groups, count, rows, width), jnp.bfloat16)
    big = jax.ShapeDtypeStruct(grad.shape, jnp.float32)
    extra = [] if held is None else list(held)
    return pl.pallas_call(
        functools.partial(update_kernel, (send, keep)),
        grid=(groups,),
        in_specs=[
            pl.BlockSpec(memory_space=pltpu.SMEM),
            pl.BlockSpec((1, depth, 128), lambda g: (g, 0, 0)),
            pl.BlockSpec((pl.Element(1), pl.Element(1), pl.Element(width)), cols),
            whole,
            whole,
            *[pl.BlockSpec(piece.shape, lambda g: (0, 0)) for piece in tokens],
            *[LEFT for _ in extra],
        ],
        out_specs=[whole, whole, part(len(send)), part(len(keep))],
        out_shape=[big, big, out(len(send)), out(len(keep))],
        scratch_shapes=[pltpu.VMEM((depth, width), jnp.bfloat16)],
        input_output_aliases={5 + count: 0, 6 + count: 1} if extra else {},
        compiler_params=pltpu.CompilerParams(vmem_limit_bytes=max(LIMIT, (LIMIT >> 9) * width)),
        cost_estimate=pl.CostEstimate(
            flops=2 * count * rows * depth * width * groups,
            bytes_accessed=groups * width * (16 * depth + 2 * count * rows),
            transcendentals=0,
        ),
        name="update_chunk",
    )(coef, row, col, far(grad), far(weight), *tokens, *extra)


def spread_kernel(factor_ref, row_ref):
    groups, depth = factor_ref.shape
    for group in range(groups):
        for start in range(0, depth, 128):
            factor = lax.rsqrt(factor_ref[group : group + 1, start : start + 128])
            row_ref[group, start : start + 128, :] = jnp.broadcast_to(factor, (128, 128)).T


def spread_rows(factor):
    shape = (*factor.shape, 128)
    return pl.pallas_call(
        spread_kernel,
        in_specs=[WHOLE],
        out_specs=WHOLE,
        out_shape=jax.ShapeDtypeStruct(shape, jnp.float32),
        compiler_params=pltpu.CompilerParams(vmem_limit_bytes=LIMIT),
        cost_estimate=pl.CostEstimate(flops=0, bytes_accessed=512 * factor.size, transcendentals=0),
        name="spread_rows",
    )(factor)


def combine_kernel(count, *refs):
    refs[-1][...] = sum(ref[...].astype(jnp.float32) for ref in refs[:count]).astype(jnp.bfloat16)


def combine(terms, blocks):
    groups, _, rows, width = terms[0][0].shape

    def pick(names):
        places = [names.index(block) for block in blocks]
        place = lambda b: functools.reduce(lambda rest, i: jnp.where(b == i, places[i], rest), range(1, len(places)), places[0])
        return pl.BlockSpec((1, 1, rows, width), lambda g, b: (g, place(b), 0, 0))

    return pl.pallas_call(
        functools.partial(combine_kernel, len(terms)),
        grid=(groups, len(blocks)),
        in_specs=[pick(names) for _, names in terms],
        out_specs=pl.BlockSpec((1, 1, rows, width), lambda g, b: (g, b, 0, 0)),
        out_shape=jax.ShapeDtypeStruct((groups, len(blocks), rows, width), jnp.bfloat16),
        compiler_params=pltpu.CompilerParams(vmem_limit_bytes=LIMIT),
        cost_estimate=pl.CostEstimate(
            flops=0, bytes_accessed=2 * (len(terms) + 1) * groups * len(blocks) * rows * width, transcendentals=0
        ),
        name="combine",
    )(*[value for value, _ in terms])


def final_kernel(counts, *refs):
    out_ref, place, start = refs[-1], 0, 0
    for count in counts:
        terms = refs[place : place + count]
        gate, up = [sum(ref[g, 0].astype(jnp.float32) for ref in terms) for g in range(2)]
        width = gate.shape[1]
        out_ref[:, start : start + width] = (jax.nn.gelu(gate, approximate=True) * up).astype(out_ref.dtype)
        place, start = place + count, start + width


def finish(chunks, hidden, start, shape):
    rows = shape[0]
    columns = sum(terms[0][0].shape[3] for terms in chunks)
    height = rows // 2
    terms = [term for chunk in chunks for term in chunk]
    spec = lambda value, place: pl.BlockSpec((2, 1, height, value.shape[3]), lambda i: (0, place, i, 0))
    extra = [] if hidden is None else [hidden]
    return pl.pallas_call(
        functools.partial(final_kernel, [len(chunk) for chunk in chunks]),
        grid=(rows // height,),
        in_specs=[spec(value, place) for value, place in terms] + [LEFT for _ in extra],
        out_specs=pl.BlockSpec((pl.Element(height), pl.Element(columns)), lambda i: (i * height, start)),
        out_shape=jax.ShapeDtypeStruct(shape, jnp.bfloat16),
        input_output_aliases={len(terms): 0} if extra else {},
        compiler_params=pltpu.CompilerParams(vmem_limit_bytes=LIMIT),
        cost_estimate=pl.CostEstimate(flops=0, bytes_accessed=20 * rows * columns, transcendentals=rows * columns),
        name="finish",
    )(*[value for value, _ in terms], *extra)


def plan(columns, count):
    bits = bits_of(count)
    units = columns // 128
    widths = [units // 4, units * 3 // 16, units - 2 * (units // 4) - units * 3 // 16, units // 4]
    if units % 16 or len(bits) < 2:
        widths = [units - units // 2, units // 2]
    chunks, start = [], 0
    for i, width in enumerate(widths):
        turn = i % max(1, len(bits))
        if width:
            chunks.append((start * 128, width * 128, bits[turn:] + bits[:turn]))
        start += width
    return chunks


def split(blocks, bit):
    return [b for b in blocks if b & bit], [b for b in blocks if not b & bit]


def program(
    tokens, inner_weight, inner_grad, inner_row, inner_col, outer_weight, outer_grad, outer_row, outer_col
):
    data_count = lax.axis_size("dp")
    data_index = lax.axis_index("dp")
    groups, depth, columns = inner_grad.shape
    rows = tokens.shape[0]
    sum_data = lambda v: total(v, "dp", rounds("dp", (4,)))
    sum_model = lambda v: total(v, "mp", rounds("mp", (2,)))

    col_part = statistics(functools.partial(col_kernel, 1e-30), (inner_grad,), (), (groups, columns), ())
    col_sum = sum_data(col_part)
    inner_col_new = FORGET * inner_col + FRESH * (col_sum / D)
    inverse_col = 1.0 / inner_col_new
    tokens_late = tie(tokens, col_part)
    share = []
    for flip in range(data_count):
        if flip:
            piece = lax.dynamic_slice_in_dim(tokens_late, (data_index ^ flip) * depth, depth, 1)
            share.append(swap(piece, "dp", flip))

    columned = [pltpu.VMEM((depth, 128), jnp.float32)] * 2
    packed = statistics(row_kernel, (inner_grad, inner_weight), (inverse_col,), (groups, 2 * depth + 128), columned)
    share = [lax.dynamic_slice_in_dim(tie(tokens, packed), data_index * depth, depth, 1), *share]
    outer_grad = tie(outer_grad, packed)
    outer_sq = outer_grad * outer_grad
    outer_part = jnp.sum(outer_sq + 1e-30, axis=1)
    packed = sum_model(packed)
    row_sum, weighted, weight_sq = packed[:, :depth], packed[:, depth : 2 * depth], packed[:, 2 * depth]
    inner_row_new = FORGET * inner_row + FRESH * (row_sum / FF)
    scalars = jnp.stack([jnp.sum(inner_row_new, 1), jnp.sum(weighted / inner_row_new, 1), weight_sq], 1)
    scalars = jnp.broadcast_to(scalars[:, :, None], (groups, 3, 128)).reshape(-1)
    scalars = sum_data(jnp.concatenate([outer_part, scalars]))
    outer_row_sum = scalars[: outer_part.size]
    scalars = scalars[outer_part.size :].reshape(groups, 3, 128)[:, :, 0]
    mean = scalars[:, 0] / D
    clip = jnp.maximum(1.0, jnp.sqrt(mean * scalars[:, 1] / (D * FF)))
    step = RELATIVE * jnp.sqrt(scalars[:, 2] / (D * FF))
    coef = -(step / clip) * jnp.sqrt(mean)
    row = spread_rows(inner_row_new)
    col = lax.rsqrt(inner_col_new)[:, None, :]

    held, chunks = None, []
    for start, width, order in plan(columns, data_count):
        send, keep = split(list(range(data_count)), order[0])
        *held, sent, kept = update_chunk(
            coef, share, row, col, inner_grad, inner_weight, held, start, width, send, keep
        )
        came = swap(sent, "dp", order[0])
        chunks.append((start, width, order, keep, [(kept, keep), (came, keep)]))
    inner_new, inner_update = held

    for level in range(1, len(bits_of(data_count))):
        later = []
        for start, width, order, blocks, terms in chunks:
            send, keep = split(blocks, order[level])
            sent = combine(terms, send)
            came = swap(sent, "dp", order[level])
            later.append((start, width, order, keep, [*terms, (came, keep)]))
        chunks = later
    hidden, half = None, len(chunks) // 2
    for group in (chunks[:half], chunks[half:]):
        if group:
            terms = [[(value, names.index(0)) for value, names in terms] for *_, terms in group]
            hidden = finish(terms, hidden, group[0][0], (rows, columns))

    outer_row_new = FORGET * outer_row + FRESH * (outer_row_sum / D)
    outer_grad, outer_weight = tie(outer_grad, outer_row_new), tie(outer_weight, outer_row_new)
    depth, columns = outer_grad.shape
    spread = (pltpu.VMEM((depth, 128), jnp.float32),)
    bigs = (outer_grad[None], outer_weight[None])
    packed = statistics(outer_kernel, bigs, (outer_row_new[None],), (1, 2 * columns + 256), spread)
    packed = sum_model(packed)[0]
    width = outer_col.shape[0]
    outer_col_new = FORGET * outer_col + FRESH * (packed[:width] / FF)
    scalars = jnp.stack([jnp.sum(packed[width : 2 * width] / outer_col_new), packed[2 * width]])
    scalars = sum_data(jnp.broadcast_to(scalars[:, None], (2, 128)))[:, 0]
    mean = packed[2 * width + 128] / FF
    clip = jnp.maximum(1.0, jnp.sqrt(mean * scalars[0] / (D * FF)))
    step = RELATIVE * jnp.sqrt(scalars[1] / (D * FF))
    scale = -(step / clip) * jnp.sqrt(mean)
    outer_update = outer_grad * (lax.rsqrt(outer_row_new)[:, None] * (lax.rsqrt(outer_col_new) * scale)[None, :])
    outer_new = outer_weight + outer_update
    return (
        inner_new,
        inner_update,
        inner_row_new,
        inner_col_new,
        outer_new,
        outer_update,
        outer_row_new,
        outer_col_new,
        hidden,
    )


def solution(mesh):
    placed = (
        P("dp", None),
        P(None, "dp", "mp"),
        P(None, "dp", "mp"),
        P(None, "dp"),
        P(None, "mp"),
        P("mp", "dp"),
        P("mp", "dp"),
        P("mp"),
        P("dp"),
    )
    return jax.shard_map(
        program,
        mesh=mesh,
        in_specs=placed,
        out_specs=(
            P(None, "dp", "mp"),
            P(None, "dp", "mp"),
            P(None, "dp"),
            P(None, "mp"),
            P("mp", "dp"),
            P("mp", "dp"),
            P("mp"),
            P("dp"),
            P("dp", "mp"),
        ),
        check_vma=False,
    )
```
